32 devices in a mesh: slab: 8 (over y, x, core), grp: 4 (over z).
Axes of the slice: x: 2, y: 2, z: 4, core: 2. Of those that a mesh axis runs over, the one named last changes fastest.
Arguments:
- near_field: bfloat16 [2, 4096, 2048], P(None, 'slab', 'grp'), may hold values from -6 to 6
- lens_phase: float32 [2, 4096, 2048], P(None, 'slab', 'grp'), may hold values from -3.140625 to 3.140625
Outputs:
- far_field: float32 [2, 512, 2048], P(None, ('slab', 'grp'))
The draws below stay inside these ranges and needn't reach their ends.
All inputs are finite; a program needn't handle non-finite values.
Results may differ from the reference program's by a relative error of at most 0.0083.
Values may be sent and summed in bfloat16 or wider, within the bound.
A program may use at most 128 MiB of HBM per device.

```python
import math
import jax
import jax.numpy as jnp
from jax import lax

NV = 2048
AV = 512
AL = 2048
STEPS = 2
LAT_DEV = 512
NL = 4096
N_SLAB = 8


def level_of(stream_key, shape, split, smallest, high):
    level = 1.0
    for dim, parts in split:
        heights = jax.random.uniform(jax.random.fold_in(jax.random.fold_in(stream_key, 6), dim), (parts,), jnp.float32, smallest / len(split), high / len(split))
        level = level * jnp.repeat(jnp.exp(heights), shape[dim] // parts).reshape((-1,) + (1,) * (len(shape) - 1 - dim))
    return level


def normal_values(own_key, shape, deviation, bound, shards=(), kind=jnp.bfloat16):
    level = level_of(own_key, shape, shards, -0.22, 0.18) if shards else 1.0
    result = jax.random.normal(own_key, shape, jnp.float32) * deviation * level
    return jnp.minimum(jnp.maximum(result, -bound), bound).astype(kind)


def setup_inputs(seed: int = 0) -> dict:
    splits = jax.random.split(jax.random.key(seed), 3)
    return {
        "near_field": normal_values(splits[0], (2, NL, NV), 1.0, 6.0, ((1, 8), (2, 4))),
        "lens_phase": jnp.clip(jax.random.uniform(splits[1], (STEPS, NL, NV), jnp.float32, -3.140625, 3.140625), -3.140625, 3.140625),
    }


def phase_table(row_index, col_index, modulus):
    turns = jnp.mod(row_index[:, None] * col_index[None, :], modulus)
    angle = turns.astype(jnp.float32) * (2.0 * math.pi / modulus)
    return (jnp.cos(angle).astype(jnp.bfloat16), jnp.sin(angle).astype(jnp.bfloat16))

def propagator():
    wave_index = jnp.arange(NV, dtype=jnp.int32)
    offset = wave_index[None, :] - wave_index[:, None]
    turns = jnp.mod(offset * offset, 2 * NV)
    angle = turns.astype(jnp.float32) * (math.pi / NV) - math.pi / 4.0
    gain = 1.0 / math.sqrt(NV)
    return ((jnp.cos(angle) * gain).astype(jnp.bfloat16), (jnp.sin(angle) * gain).astype(jnp.bfloat16))

def matmul(left, right):
    return jnp.dot(left.astype(jnp.float32), right.astype(jnp.float32), precision=lax.Precision.HIGHEST)

def reference(near_field, lens_phase):
    total_rows = LAT_DEV * N_SLAB
    wave_index = jnp.arange(NV, dtype=jnp.int32)
    prop_cos, prop_sin = propagator()
    real_part = near_field[0]
    imag_part = near_field[1]
    for section in range(STEPS):
        prop_real = (matmul(real_part, prop_cos) - matmul(imag_part, prop_sin)).astype(jnp.bfloat16)
        prop_imag = (matmul(real_part, prop_sin) + matmul(imag_part, prop_cos)).astype(jnp.bfloat16)
        lens_cos = jnp.cos(lens_phase[section])
        lens_sin = jnp.sin(lens_phase[section])
        prop_real = prop_real.astype(jnp.float32)
        prop_imag = prop_imag.astype(jnp.float32)
        real_part = (prop_real * lens_cos - prop_imag * lens_sin).astype(jnp.bfloat16)
        imag_part = (prop_real * lens_sin + prop_imag * lens_cos).astype(jnp.bfloat16)
    vert_cos, vert_sin = phase_table(wave_index - NV // 2, jnp.arange(AV, dtype=jnp.int32) - AV // 2, 2 * NV)
    col_real = (matmul(real_part, vert_cos) + matmul(imag_part, vert_sin)).astype(jnp.bfloat16)
    col_imag = (matmul(imag_part, vert_cos) - matmul(real_part, vert_sin)).astype(jnp.bfloat16)
    lat_cos, lat_sin = phase_table(jnp.arange(total_rows, dtype=jnp.int32) - total_rows // 2, jnp.arange(AL, dtype=jnp.int32) - AL // 2, 2 * total_rows)
    lat_cos = lat_cos.astype(jnp.float32)
    lat_sin = lat_sin.astype(jnp.float32)
    col_real = col_real.astype(jnp.float32)
    col_imag = col_imag.astype(jnp.float32)
    hp = lax.Precision.HIGHEST
    out_real = jnp.einsum('na,nj->aj', col_real, lat_cos, precision=hp) + jnp.einsum('na,nj->aj', col_imag, lat_sin, precision=hp)
    out_imag = jnp.einsum('na,nj->aj', col_imag, lat_cos, precision=hp) - jnp.einsum('na,nj->aj', col_real, lat_sin, precision=hp)
    scale = 1.0 / math.sqrt(total_rows * NV)
    return jnp.stack([out_real, out_imag]) * scale
```

```python
import math

import jax
import jax.numpy as jnp
from jax import lax
from jax.sharding import PartitionSpec as P

AV = 512
AL = 2048
PHASE_CODE = 40.0


def sincos(angle):
    half = 0.5 * angle
    sq = half * half
    sin = -1.0 / 39916800.0
    for term in (1.0 / 362880.0, -1.0 / 5040.0, 1.0 / 120.0, -1.0 / 6.0, 1.0):
        sin = sin * sq + term
    sin = sin * half
    cos = 1.0 / 479001600.0
    for term in (-1.0 / 3628800.0, 1.0 / 40320.0, -1.0 / 720.0, 1.0 / 24.0, -0.5, 1.0):
        cos = cos * sq + term
    return 1.0 - 2.0 * sin * sin, 2.0 * sin * cos


def unit_angle(turns, modulus):
    assert modulus & (modulus - 1) == 0
    centred = ((turns + modulus // 2) & (modulus - 1)) - modulus // 2
    return sincos(centred.astype(jnp.float32) * (2.0 * math.pi / modulus))


def count(size):
    return lax.optimization_barrier(jnp.arange(size, dtype=jnp.int32))


def phase_table(row_index, col_index, modulus):
    cos, sin = unit_angle(row_index[:, None] * col_index[None, :], modulus)
    return cos.astype(jnp.bfloat16), sin.astype(jnp.bfloat16)


def propagator(points):
    band = math.gcd(points, 128)
    offset = count(points)[None, :] - count(band)[:, None]
    cos, sin = unit_angle(offset * offset - points // 4, 2 * points)
    gain = 1.0 / math.sqrt(points)

    def rolled(part):
        part = lax.optimization_barrier((part * gain).astype(jnp.bfloat16))
        twice = jnp.concatenate([part, part], axis=1)
        return jnp.concatenate(
            [
                lax.slice_in_dim(twice, points - start, 2 * points - start, axis=1)
                for start in range(0, points, band)
            ]
        )

    return rolled(cos), rolled(sin)


def matmul(left, right):
    return jnp.dot(left, right, preferred_element_type=jnp.float32)


def complex_product(both, table_cos, table_sin):
    rows = both.shape[0] // 2
    with_cos = matmul(both, table_cos)
    with_sin = matmul(both, table_sin)
    return with_cos[:rows] - with_sin[rows:], with_sin[:rows] + with_cos[rows:]


def on_device(near_field, lens_phase):
    slab_count = lax.axis_size("slab")
    group_count = lax.axis_size("grp")
    devices = slab_count * group_count
    steps, lat_dev, width = lens_phase.shape
    points = width * group_count
    total_rows = lat_dev * slab_count
    rows = lat_dev // group_count
    angles = AV // devices
    coded = [jnp.exp2(lens_phase[k] * PHASE_CODE).astype(jnp.bfloat16) for k in range(steps)]
    field = lax.all_to_all(near_field, "grp", split_axis=1, concat_axis=2, tiled=True)
    coded = [
        lax.all_to_all(part, "grp", split_axis=0, concat_axis=1, tiled=True) for part in coded
    ]
    prop_cos, prop_sin = propagator(points)
    both = field.reshape(2 * rows, points)
    for section in range(steps):
        real, imag = complex_product(both, prop_cos, prop_sin)
        real = real.astype(jnp.bfloat16).astype(jnp.float32)
        imag = imag.astype(jnp.bfloat16).astype(jnp.float32)
        phase = jnp.log2(coded[section].astype(jnp.float32)) * (1.0 / PHASE_CODE)
        lens_cos, lens_sin = sincos(phase)
        both = jnp.concatenate(
            [
                (real * lens_cos - imag * lens_sin).astype(jnp.bfloat16),
                (real * lens_sin + imag * lens_cos).astype(jnp.bfloat16),
            ]
        )
    vert_cos, vert_sin = phase_table(
        count(points) - points // 2,
        count(AV) - AV // 2,
        2 * points,
    )
    col_real, col_imag = complex_product(both, vert_cos, -vert_sin)
    cols = jnp.stack([col_real, col_imag]).astype(jnp.bfloat16)
    cols = jnp.transpose(cols.reshape(2, rows, devices, angles), (2, 0, 3, 1))
    got = lax.all_to_all(cols, ("slab", "grp"), split_axis=0, concat_axis=0, tiled=True)
    modulus = 2 * total_rows
    period = modulus // rows
    source = count(devices) - devices // 2
    fine = count(period)
    near = count(rows)
    coarse = count(AL // period)
    w_cos, w_sin = phase_table(source, fine, period)
    got_real = got[:, 0]
    got_imag = got[:, 1]
    ein = lambda s, l, r: jnp.einsum(s, l, r, preferred_element_type=jnp.float32)
    mid_real = ein("sam,sf->afm", got_real, w_cos) + ein("sam,sf->afm", got_imag, w_sin)
    mid_imag = ein("sam,sf->afm", got_imag, w_cos) - ein("sam,sf->afm", got_real, w_sin)
    t_cos, t_sin = unit_angle(fine[:, None] * near[None, :], modulus)
    turned_real = (mid_real * t_cos + mid_imag * t_sin).astype(jnp.bfloat16)
    turned_imag = (mid_imag * t_cos - mid_real * t_sin).astype(jnp.bfloat16)
    e_cos, e_sin = phase_table(near, coarse * period - AL // 2, modulus)
    out_real = ein("afm,mc->acf", turned_real, e_cos) + ein("afm,mc->acf", turned_imag, e_sin)
    out_imag = ein("afm,mc->acf", turned_imag, e_cos) - ein("afm,mc->acf", turned_real, e_sin)
    scale = 1.0 / math.sqrt(total_rows * points)
    return (jnp.stack([out_real, out_imag]) * scale).reshape(2, angles, AL)


def solution(mesh):
    return jax.shard_map(
        on_device,
        mesh=mesh,
        in_specs=(P(None, "slab", "grp"), P(None, "slab", "grp")),
        out_specs=P(None, ("slab", "grp"), None),
        check_vma=False,
    )
```

```python
import math

import jax
import jax.numpy as jnp
from jax import lax
from jax.experimental import pallas as pl
from jax.experimental.pallas import tpu as pltpu
from jax.sharding import PartitionSpec as P

AV = 512
AL = 2048
PHASE_CODE = 40.0


def sincos(angle):
    half = 0.5 * angle
    sq = half * half
    sin = -1.0 / 39916800.0
    for term in (1.0 / 362880.0, -1.0 / 5040.0, 1.0 / 120.0, -1.0 / 6.0, 1.0):
        sin = sin * sq + term
    sin = sin * half
    cos = 1.0 / 479001600.0
    for term in (-1.0 / 3628800.0, 1.0 / 40320.0, -1.0 / 720.0, 1.0 / 24.0, -0.5, 1.0):
        cos = cos * sq + term
    return 1.0 - 2.0 * sin * sin, 2.0 * sin * cos


def unit_angle(turns, modulus):
    assert modulus & (modulus - 1) == 0
    centred = ((turns + modulus // 2) & (modulus - 1)) - modulus // 2
    return sincos(centred.astype(jnp.float32) * (2.0 * math.pi / modulus))


def count(size):
    return lax.optimization_barrier(jnp.arange(size, dtype=jnp.int32))


def phase_table(row_index, col_index, modulus):
    cos, sin = unit_angle(row_index[:, None] * col_index[None, :], modulus)
    return cos.astype(jnp.bfloat16), sin.astype(jnp.bfloat16)


def propagator(points):
    band = math.gcd(points, 256)
    offset = count(points)[None, :] - count(band)[:, None]
    cos, sin = unit_angle(offset * offset - points // 4, 2 * points)
    gain = 1.0 / math.sqrt(points)

    def rolled(part):
        part = lax.optimization_barrier((part * gain).astype(jnp.bfloat16))
        twice = jnp.concatenate([part, part], axis=1)
        return jnp.concatenate(
            [
                lax.slice_in_dim(twice, points - start, 2 * points - start, axis=1)
                for start in range(0, points, band)
            ]
        )

    return rolled(cos), rolled(sin)


def matmul(left, right):
    return jnp.dot(left, right, preferred_element_type=jnp.float32)


def complex_product(both, table_cos, table_sin):
    rows = both.shape[0] // 2
    with_cos = matmul(both, table_cos)
    with_sin = matmul(both, table_sin)
    return with_cos[:rows] - with_sin[rows:], with_sin[:rows] + with_cos[rows:]


def exchange_kernel(groups, devices, source, target, send_sem, recv_sem, own_sem):
    me = lax.axis_index("slab") * groups + lax.axis_index("grp")
    barrier = pltpu.get_barrier_semaphore()

    def place(device):
        return (lax.div(device, groups), lax.rem(device, groups))

    def greet(step, carry):
        peer = lax.rem(me + step, devices)
        pl.semaphore_signal(
            barrier, inc=1, device_id=place(peer), device_id_type=pl.DeviceIdType.MESH
        )
        return carry

    lax.fori_loop(1, devices, greet, 0)
    pl.semaphore_wait(barrier, devices - 1)

    def block(step):
        peer = lax.rem(me + step, devices)
        return pltpu.make_async_remote_copy(
            src_ref=source.at[peer],
            dst_ref=target.at[me],
            send_sem=send_sem.at[step],
            recv_sem=recv_sem.at[step],
            device_id=place(peer),
            device_id_type=pl.DeviceIdType.MESH,
        )

    def send(step, carry):
        block(step).start()
        return carry

    def wait(step, carry):
        block(step).wait()
        return carry

    lax.fori_loop(1, devices, send, 0)
    own = pltpu.make_async_copy(source.at[me], target.at[me], own_sem)
    own.start()
    own.wait()
    lax.fori_loop(1, devices, wait, 0)


def exchange(blocks, groups):
    devices = blocks.shape[0]

    def kernel(*refs):
        exchange_kernel(groups, devices, *refs)

    return pl.pallas_call(
        kernel,
        out_shape=jax.ShapeDtypeStruct(blocks.shape, blocks.dtype),
        in_specs=[pl.BlockSpec(memory_space=pltpu.VMEM)],
        out_specs=pl.BlockSpec(memory_space=pltpu.VMEM),
        scratch_shapes=[
            pltpu.SemaphoreType.DMA((devices,)),
            pltpu.SemaphoreType.DMA((devices,)),
            pltpu.SemaphoreType.DMA,
        ],
        compiler_params=pltpu.CompilerParams(collective_id=0, has_side_effects=True),
        name="column_exchange",
    )(blocks)


def on_device(near_field, lens_phase):
    slab_count = lax.axis_size("slab")
    group_count = lax.axis_size("grp")
    devices = slab_count * group_count
    steps, lat_dev, width = lens_phase.shape
    points = width * group_count
    total_rows = lat_dev * slab_count
    rows = lat_dev // group_count
    angles = AV // devices
    coded = [jnp.exp2(lens_phase[k] * PHASE_CODE).astype(jnp.bfloat16) for k in range(steps)]
    field = lax.all_to_all(near_field, "grp", split_axis=1, concat_axis=2, tiled=True)
    arrived = field
    moved = []
    for part in coded:
        part, arrived = lax.optimization_barrier((part, arrived))
        if not moved:
            field = arrived
        else:
            moved[-1] = arrived
        arrived = lax.all_to_all(part, "grp", split_axis=0, concat_axis=1, tiled=True)
        moved.append(arrived)
    coded = moved
    prop_cos, prop_sin = propagator(points)
    both = field.reshape(2 * rows, points)
    for section in range(steps):
        real, imag = complex_product(both, prop_cos, prop_sin)
        real = real.astype(jnp.bfloat16).astype(jnp.float32)
        imag = imag.astype(jnp.bfloat16).astype(jnp.float32)
        phase = jnp.log2(coded[section].astype(jnp.float32)) * (1.0 / PHASE_CODE)
        lens_cos, lens_sin = sincos(phase)
        both = jnp.concatenate(
            [
                (real * lens_cos - imag * lens_sin).astype(jnp.bfloat16),
                (real * lens_sin + imag * lens_cos).astype(jnp.bfloat16),
            ]
        )
    vert_cos, vert_sin = phase_table(
        count(points) - points // 2,
        count(AV) - AV // 2,
        2 * points,
    )
    vert_cos, vert_sin = lax.optimization_barrier((vert_cos, -vert_sin))
    col_real, col_imag = complex_product(both, vert_cos, vert_sin)
    cols = jnp.stack([col_real, col_imag]).astype(jnp.bfloat16)
    cols = jnp.transpose(cols.reshape(2, rows, devices, angles), (2, 0, 3, 1))
    got = exchange(cols.reshape(devices, 2 * angles, rows), group_count)
    got = got.reshape(devices, 2, angles, rows)
    modulus = 2 * total_rows
    period = modulus // rows
    source = count(devices) - devices // 2
    fine = count(period)
    near = count(rows)
    coarse = count(AL // period)
    w_cos, w_sin = phase_table(source, fine, period)
    got_real = got[:, 0]
    got_imag = got[:, 1]
    ein = lambda s, l, r: jnp.einsum(s, l, r, preferred_element_type=jnp.float32)
    mid_real = ein("sam,sf->afm", got_real, w_cos) + ein("sam,sf->afm", got_imag, w_sin)
    mid_imag = ein("sam,sf->afm", got_imag, w_cos) - ein("sam,sf->afm", got_real, w_sin)
    t_cos, t_sin = unit_angle(fine[:, None] * near[None, :], modulus)
    turned_real = (mid_real * t_cos + mid_imag * t_sin).astype(jnp.bfloat16)
    turned_imag = (mid_imag * t_cos - mid_real * t_sin).astype(jnp.bfloat16)
    e_cos, e_sin = phase_table(near, coarse * period - AL // 2, modulus)
    out_real = ein("afm,mc->acf", turned_real, e_cos) + ein("afm,mc->acf", turned_imag, e_sin)
    out_imag = ein("afm,mc->acf", turned_imag, e_cos) - ein("afm,mc->acf", turned_real, e_sin)
    scale = 1.0 / math.sqrt(total_rows * points)
    return (jnp.stack([out_real, out_imag]) * scale).reshape(2, angles, AL)


def solution(mesh):
    return jax.shard_map(
        on_device,
        mesh=mesh,
        in_specs=(P(None, "slab", "grp"), P(None, "slab", "grp")),
        out_specs=P(None, ("slab", "grp"), None),
        check_vma=False,
    )
```

```python
import math

import jax
import jax.numpy as jnp
from jax import lax
from jax.experimental import pallas as pl
from jax.experimental.pallas import tpu as pltpu
from jax.sharding import PartitionSpec as P

AV = 512
AL = 2048
PHASE_CODE = 40.0


def sincos(angle):
    half = 0.5 * angle
    sq = half * half
    sin = -1.0 / 39916800.0
    for term in (1.0 / 362880.0, -1.0 / 5040.0, 1.0 / 120.0, -1.0 / 6.0, 1.0):
        sin = sin * sq + term
    sin = sin * half
    cos = 1.0 / 479001600.0
    for term in (-1.0 / 3628800.0, 1.0 / 40320.0, -1.0 / 720.0, 1.0 / 24.0, -0.5, 1.0):
        cos = cos * sq + term
    return 1.0 - 2.0 * sin * sin, 2.0 * sin * cos


def unit_angle(turns, modulus):
    assert modulus & (modulus - 1) == 0
    centred = ((turns + modulus // 2) & (modulus - 1)) - modulus // 2
    return sincos(centred.astype(jnp.float32) * (2.0 * math.pi / modulus))


def count(size):
    return lax.optimization_barrier(jnp.arange(size, dtype=jnp.int32))


def phase_table(row_index, col_index, modulus):
    cos, sin = unit_angle(row_index[:, None] * col_index[None, :], modulus)
    return cos.astype(jnp.bfloat16), sin.astype(jnp.bfloat16)


def conjugate(table):
    cos, sin = table
    return jnp.stack([jnp.stack([cos, -sin]), jnp.stack([sin, cos])])


def propagator(points):
    band = math.gcd(points, 256)
    offset = count(points)[None, :] - count(band)[:, None]
    cos, sin = unit_angle(offset * offset - points // 4, 2 * points)
    gain = 1.0 / math.sqrt(points)

    def rolled(part):
        part = lax.optimization_barrier((part * gain).astype(jnp.bfloat16))
        twice = jnp.concatenate([part, part], axis=1)
        return jnp.concatenate(
            [
                lax.slice_in_dim(twice, points - start, 2 * points - start, axis=1)
                for start in range(0, points, band)
            ]
        )

    return rolled(cos), rolled(sin)


def matmul(left, right):
    return jnp.dot(left, right, preferred_element_type=jnp.float32)


def complex_product(both, table_cos, table_sin):
    rows = both.shape[0] // 2
    with_cos = matmul(both, table_cos)
    with_sin = matmul(both, table_sin)
    return with_cos[:rows] - with_sin[rows:], with_sin[:rows] + with_cos[rows:]


def exchange_kernel(groups, devices, source, target, send_sem, recv_sem, own_sem):
    me = lax.axis_index("slab") * groups + lax.axis_index("grp")
    barrier = pltpu.get_barrier_semaphore()

    def place(device):
        return (lax.div(device, groups), lax.rem(device, groups))

    def greet(step, carry):
        peer = lax.rem(me + step, devices)
        pl.semaphore_signal(
            barrier, inc=1, device_id=place(peer), device_id_type=pl.DeviceIdType.MESH
        )
        return carry

    lax.fori_loop(1, devices, greet, 0)
    pl.semaphore_wait(barrier, devices - 1)

    def block(step):
        peer = lax.rem(me + step, devices)
        return pltpu.make_async_remote_copy(
            src_ref=source.at[peer],
            dst_ref=target.at[me],
            send_sem=send_sem.at[step],
            recv_sem=recv_sem.at[step],
            device_id=place(peer),
            device_id_type=pl.DeviceIdType.MESH,
        )

    def send(step, carry):
        block(step).start()
        return carry

    def wait(step, carry):
        block(step).wait()
        return carry

    lax.fori_loop(1, devices, send, 0)
    own = pltpu.make_async_copy(source.at[me], target.at[me], own_sem)
    own.start()
    own.wait()
    lax.fori_loop(1, devices, wait, 0)


def exchange(blocks, groups):
    devices = blocks.shape[0]

    def kernel(*refs):
        exchange_kernel(groups, devices, *refs)

    return pl.pallas_call(
        kernel,
        out_shape=jax.ShapeDtypeStruct(blocks.shape, blocks.dtype),
        in_specs=[pl.BlockSpec(memory_space=pltpu.VMEM)],
        out_specs=pl.BlockSpec(memory_space=pltpu.VMEM),
        scratch_shapes=[
            pltpu.SemaphoreType.DMA((devices,)),
            pltpu.SemaphoreType.DMA((devices,)),
            pltpu.SemaphoreType.DMA,
        ],
        compiler_params=pltpu.CompilerParams(collective_id=0, has_side_effects=True),
        name="column_exchange",
    )(blocks)


def on_device(near_field, lens_phase):
    slab_count = lax.axis_size("slab")
    group_count = lax.axis_size("grp")
    devices = slab_count * group_count
    steps, lat_dev, width = lens_phase.shape
    points = width * group_count
    total_rows = lat_dev * slab_count
    rows = lat_dev // group_count
    angles = AV // devices
    coded = [jnp.exp2(lens_phase[k] * PHASE_CODE).astype(jnp.bfloat16) for k in range(steps)]
    blocks = jnp.transpose(near_field.reshape(2, group_count, rows, width), (1, 0, 2, 3))
    field = lax.all_to_all(blocks, "grp", split_axis=0, concat_axis=0, tiled=True)
    arrived = field
    moved = []
    for part in coded:
        part, arrived = lax.optimization_barrier((part, arrived))
        if not moved:
            field = arrived
        else:
            moved[-1] = arrived
        arrived = lax.all_to_all(part, "grp", split_axis=0, concat_axis=1, tiled=True)
        moved.append(arrived)
    coded = moved
    prop_cos, prop_sin = propagator(points)
    both = jnp.transpose(field, (1, 2, 0, 3)).reshape(2 * rows, points)
    for section in range(steps):
        real, imag = complex_product(both, prop_cos, prop_sin)
        real = real.astype(jnp.bfloat16).astype(jnp.float32)
        imag = imag.astype(jnp.bfloat16).astype(jnp.float32)
        phase = jnp.log2(coded[section].astype(jnp.float32)) * (1.0 / PHASE_CODE)
        lens_cos, lens_sin = sincos(phase)
        both = jnp.concatenate(
            [
                (real * lens_cos - imag * lens_sin).astype(jnp.bfloat16),
                (real * lens_sin + imag * lens_cos).astype(jnp.bfloat16),
            ]
        )
    vert_cos, vert_sin = phase_table(
        count(AV) - AV // 2, count(points) - points // 2, 2 * points
    )
    vert_cos, vert_sin = lax.optimization_barrier((vert_cos, vert_sin))
    with_cos = jnp.einsum("av,nv->an", vert_cos, both, preferred_element_type=jnp.float32)
    with_sin = jnp.einsum("av,nv->an", vert_sin, both, preferred_element_type=jnp.float32)
    col_real = (with_cos[:, :rows] + with_sin[:, rows:]).astype(jnp.bfloat16)
    col_imag = (with_cos[:, rows:] - with_sin[:, :rows]).astype(jnp.bfloat16)
    cols = jnp.stack([part.reshape(devices, angles, rows) for part in (col_real, col_imag)], axis=1)
    got = exchange(cols.reshape(devices, 2 * angles, rows), group_count)
    modulus = 2 * total_rows
    period = modulus // rows
    source = count(devices) - devices // 2
    fine = count(period)
    near = count(rows)
    coarse = count(AL // period)
    scale = 1.0 / math.sqrt(total_rows * points)
    got = got.reshape(devices, 2, angles, rows)
    weights = conjugate(phase_table(source, fine, period))
    mid = jnp.einsum("skam,kcsf->cafm", got, weights, preferred_element_type=jnp.float32)
    t_cos, t_sin = unit_angle(fine[:, None] * near[None, :], modulus)
    t_cos = t_cos * scale
    t_sin = t_sin * scale
    turned = jnp.stack([mid[0] * t_cos + mid[1] * t_sin, mid[1] * t_cos - mid[0] * t_sin])
    weights = conjugate(phase_table(near, coarse * period - AL // 2, modulus))
    out = jnp.einsum(
        "kafm,kcmd->cadf", turned.astype(jnp.bfloat16), weights, preferred_element_type=jnp.float32
    )
    return out.reshape(2, angles, AL)


def solution(mesh):
    return jax.shard_map(
        on_device,
        mesh=mesh,
        in_specs=(P(None, "slab", "grp"), P(None, "slab", "grp")),
        out_specs=P(None, ("slab", "grp"), None),
        check_vma=False,
    )
```
